512 devices in a mesh: stn: 64 (over x, z), tm: 8 (over y, core).
Axes of the slice: x: 4, y: 4, z: 16, core: 2. Of those that a mesh axis runs over, the one named last changes fastest.
Arguments:
- right_sides: bfloat16 [2048, 131072], P('tm', 'stn'), may hold values from -6 to 6
- factor_cols: bfloat16 [131072, 512], P('stn'), may hold values from -0.25 to 0.25
- diag_inverses: float32 [2, 256, 256], replicated, as said below
- panel_block: int32 [1], replicated, may hold values from 0 to 510
- decay_rate: float32 [131072], P('stn'), may hold values from 0.00048828125 to 0.1
- gaps: int32 [2048], replicated, may hold values 0 or 1
Outputs:
- filtered: bfloat16 [2048, 131072], P('tm', 'stn')
The draws below stay inside these ranges and needn't reach their ends.
Inputs may be any that keep to these rules, and one draw needn't show every extreme that they name: `diag_inverses`: each block is lower triangular with diagonal entries between 1 and 2. The two panels are rows 256 * panel_block to 256 * panel_block + 2 * 256 - 1.
All inputs are finite; a program needn't handle non-finite values.
Results may differ from the reference program's by a relative error of at most 0.001.
Values may be sent and summed in bfloat16 or wider, within the bound.
A program may use at most 64 MiB of HBM per device.

```python
import math
import jax
import jax.numpy as jnp
from jax import lax

PANEL = 256
STATIONS = 131072
TIME = 2048


def draw_diag_inverses(key, part):
    rows = lax.broadcasted_iota(jnp.int32, (2, PANEL, PANEL), 1)
    cols = lax.broadcasted_iota(jnp.int32, (2, PANEL, PANEL), 2)
    lower = jax.random.normal(jax.random.fold_in(key, 11), (2, PANEL, PANEL), jnp.float32) * (0.5 / jnp.sqrt(jnp.float32(PANEL)))
    diagonal = jax.random.uniform(jax.random.fold_in(key, 12), (2, PANEL, PANEL), jnp.float32, 1.0, 2.0)
    return jnp.where(cols < rows, lower, jnp.where(cols == rows, diagonal, 0.0)).astype(jnp.float32)


def with_ends(result, key, low, high):
    longest = result.shape.index(max(result.shape))
    spots = []
    for shift in (0, 1):
        where = [jax.random.randint(jax.random.fold_in(key, axis), (), 0, length) for axis, length in enumerate(result.shape)]
        where[longest] = (where[longest] + shift) % result.shape[longest]
        spots.append(tuple(where))
    return result.at[spots[0]].set(low).at[spots[1]].set(high)


def shard_levels(rng, extent, split, smallest, high):
    loudness = 1.0
    for position, blocks in split:
        draws = jax.random.uniform(jax.random.fold_in(jax.random.fold_in(rng, 6), position), (blocks,), jnp.float32, smallest / len(split), high / len(split))
        loudness = loudness * jnp.repeat(jnp.exp(draws), extent[position] // blocks).reshape((-1,) + (1,) * (len(extent) - 1 - position))
    return loudness


def scatter_about(own_key, extent, deviation, bound, pieces=(), kind=jnp.bfloat16):
    array = jax.random.normal(own_key, extent, jnp.float32) * deviation
    if len(pieces) > 0:
        array = shard_levels(own_key, extent, pieces, -0.22, 0.18) * array
    return jnp.clip(array, min=-bound, max=bound).astype(kind)


def setup_inputs(seed: int = 0) -> dict:
    key_list = jax.random.split(jax.random.key(seed), 7)
    return {
        "right_sides": scatter_about(key_list[0], (TIME, STATIONS), 1.0, 6.0, ((0, 8), (1, 64))),
        "factor_cols": scatter_about(key_list[1], (STATIONS, 2 * PANEL), (2 * PANEL) ** -0.5, 0.25, ((0, 64),)),
        "diag_inverses": draw_diag_inverses(jax.random.fold_in(key_list[6], 71), 0),
        "panel_block": jax.random.randint(key_list[3], (1,), 0, STATIONS // PANEL - 1).astype(jnp.int32),
        "decay_rate": jnp.clip(jnp.exp(math.log(0.1) - 5.322034 * jax.random.uniform(key_list[4], (STATIONS,), jnp.float32) ** shard_levels(key_list[4], (STATIONS,), ((0, 64),), -0.2, 0.2)), 0.00048828125, 0.1),
        "gaps": with_ends((jax.random.randint(key_list[5], (TIME,), 0, 256) < 1).astype(jnp.int32), jax.random.fold_in(key_list[5], 1), 0, 1),
    }


def reference(right_sides, factor_cols, diag_inverses, panel_block, decay_rate, gaps):
    work = right_sides.astype(jnp.float32)
    panel_rows = diag_inverses.shape[1]
    station_rows = lax.iota(jnp.int32, work.shape[1])
    start_row = (panel_block[0] * panel_rows).astype(jnp.int32)
    for which in range(2):
        first_row = start_row + which * panel_rows
        rhs_block = lax.dynamic_slice_in_dim(work, first_row, panel_rows, 1)
        solved = lax.dot_general(rhs_block, diag_inverses[which], (((1,), (1,)), ((), ())), precision=lax.Precision.HIGHEST, preferred_element_type=jnp.float32)
        work = lax.dynamic_update_slice_in_dim(work, solved, first_row, 1)
        below = (station_rows >= first_row + panel_rows).astype(jnp.float32)
        columns = factor_cols[:, which * panel_rows:(which + 1) * panel_rows].astype(jnp.float32) * below[:, None]
        work = work - lax.dot_general(solved, columns, (((1,), (1,)), ((), ())), precision=lax.Precision.HIGHEST, preferred_element_type=jnp.float32)
    rate = decay_rate
    decay = jnp.exp(-rate)
    m_aa = decay * (1.0 + rate)
    m_ab = decay
    m_ba = -decay * rate * rate
    m_bb = decay * (1.0 - rate)
    gain = 2.0 * rate * jnp.sqrt(rate)
    halving = jnp.where(gaps == 1, 0.5, 1.0).astype(jnp.float32)

    def advance(carried, element):
        inputs, factor = element
        level = carried[0] * factor
        slope = carried[1] * factor
        new_level = m_aa * level + m_ab * slope
        new_slope = m_ba * level + m_bb * slope + gain * inputs
        return ((new_level, new_slope), new_level)
    zeros_row = jnp.zeros((work.shape[1],), jnp.float32)
    _, levels = lax.scan(advance, (zeros_row, zeros_row), (work, halving))
    return levels.astype(jnp.bfloat16)
```

```python
import functools

import jax
import jax.numpy as jnp
from jax import lax
from jax.experimental import pallas as pl
from jax.experimental.pallas import tpu as pltpu
from jax.sharding import PartitionSpec as P

MESH = pl.DeviceIdType.MESH
BLK = 256
SEGS = 8
RING = 16
CHUNK = 16
F32 = jnp.float32
BF16 = jnp.bfloat16


def dot(a, b):
    return lax.dot_general(a, b, (((1,), (0,)), ((), ())), preferred_element_type=F32)


def dot_t(a, b):
    return lax.dot_general(a, b, (((1,), (1,)), ((), ())), preferred_element_type=F32)


def split3(a):
    high = a.astype(BF16)
    rest = a - high.astype(F32)
    mid = rest.astype(BF16)
    return high, mid, (rest - mid.astype(F32)).astype(BF16)


def pick_kernel(nx, pb_ref, r0_ref, r1_ref, f_ref, c_ref):
    core = lax.rem(lax.axis_index("tm"), 2)
    rows = BLK // nx
    frows = BLK // 4 // nx
    half = pl.multiple_of(core * (BLK // 2), BLK // 2)
    for q in range(nx):
        c_ref[q, 0:rows, 0:BLK] = r0_ref[rows * q : rows * (q + 1), :]
        c_ref[q, 0:rows, BLK : 2 * BLK] = r1_ref[rows * q : rows * (q + 1), :]
        for side in range(2):
            c_ref[q, rows : rows + frows, BLK * side : BLK * (side + 1)] = f_ref[
                pl.ds(half + side * (BLK // 4) + frows * q, frows), :
            ]


def pick(right_sides, factor_cols, panel_block, nx):
    blocks = right_sides.shape[1] // BLK
    piece = BLK // nx + BLK // 4 // nx
    return pl.pallas_call(
        functools.partial(pick_kernel, nx),
        out_shape=jax.ShapeDtypeStruct((nx, piece, 2 * BLK), BF16),
        grid_spec=pltpu.PrefetchScalarGridSpec(
            num_scalar_prefetch=1,
            grid=(1,),
            in_specs=[
                pl.BlockSpec((BLK, BLK), lambda i, pb: (0, lax.rem(pb[0], blocks))),
                pl.BlockSpec((BLK, BLK), lambda i, pb: (0, lax.rem(pb[0] + 1, blocks))),
                pl.BlockSpec((BLK, BLK), lambda i, pb: (lax.rem(pb[0] + 1, blocks), 0)),
            ],
            out_specs=pl.BlockSpec((nx, piece, 2 * BLK), lambda i, pb: (0, 0, 0)),
        ),
        name="pick",
    )(panel_block, right_sides, right_sides, factor_cols)


def spread_kernel(
    nx, nz, blocks, pb_ref, c_ref, p_ref, f_ref,
    xs, zs, pan, fb, own_sem, xsend, xrecv, zsend, zrecv, psend, precv, fsend, frecv,
):
    me, tm = lax.axis_index("stn"), lax.axis_index("tm")
    x, z = me // nz, lax.rem(me, nz)
    core = lax.rem(tm, 2)
    other = tm + 1 - 2 * core
    piece = c_ref.shape[1]
    rows = BLK // nx
    chunks = piece // CHUNK
    half = nz // 2
    split = (chunks + 1) // 2
    right = x * nz + lax.rem(z + 1, nz)
    left = x * nz + lax.rem(z + nz - 1, nz)

    def along_x(d):
        return lax.rem(x + d, nx) * nz + z

    barrier = pltpu.get_barrier_semaphore()
    for where in [{"stn": right}, {"stn": left}] + [
        {"stn": along_x(d), "tm": other if flip else tm}
        for flip in range(2)
        for d in range(nx)
        if flip or d
    ]:
        pl.semaphore_signal(barrier, inc=1, device_id=where, device_id_type=MESH)
    pl.semaphore_wait(barrier, 2 + 2 * nx - 1)

    own = pltpu.make_async_copy(c_ref.at[x], xs.at[0], own_sem)
    own.start()
    sends = []
    for d in range(1, nx):
        copy = pltpu.make_async_remote_copy(
            src_ref=c_ref.at[lax.rem(x + d, nx)],
            dst_ref=xs.at[d],
            send_sem=xsend.at[d],
            recv_sem=xrecv.at[d],
            device_id={"stn": along_x(d)},
            device_id_type=MESH,
        )
        copy.start()
        sends.append(copy)
    own.wait()
    for copy in sends:
        copy.wait()

    block = pb_ref[0]
    holder0 = block // blocks
    holder1 = (block + 1) // blocks
    from0 = lax.rem(x - holder0 // nz + nx, nx)
    from1 = lax.rem(x - holder1 // nz + nx, nx)
    zs[0, :, 0:BLK] = xs[from1, :, 0:BLK]
    zs[0, :, BLK : 2 * BLK] = xs[from1, :, BLK : 2 * BLK]
    zs[0, 0:rows, 0:BLK] = xs[from0, 0:rows, 0:BLK]

    def hop(way, step, c):
        src = step if way == 0 else lax.rem(nz - step, nz)
        dst = step + 1 if way == 0 else nz - 1 - step
        return pltpu.make_async_remote_copy(
            src_ref=zs.at[src, pl.ds(c * CHUNK, CHUNK), :],
            dst_ref=zs.at[dst, pl.ds(c * CHUNK, CHUNK), :],
            send_sem=zsend.at[way, step, c],
            recv_sem=zrecv.at[way, step, c],
            device_id={"stn": right if way == 0 else left},
            device_id_type=MESH,
        )

    def last(way):
        return range(split) if way == 0 else range(split, chunks)

    for c in range(chunks):
        for way in range(2):
            hop(way, 0, c).start()

    def middle(step, _):
        for c in range(chunks):
            for way in range(2):
                hop(way, step - 1, c).wait_recv()
                hop(way, step, c).start()
        return 0

    lax.fori_loop(1, half - 1, middle, 0)
    for c in range(chunks):
        for way in range(2):
            hop(way, half - 2, c).wait_recv()
            if c in last(way):
                hop(way, half - 1, c).start()
    for way in range(2):
        for c in last(way):
            hop(way, half - 1, c).wait_recv()

    back0 = lax.rem(z - lax.rem(holder0, nz) + nz, nz)
    back1 = lax.rem(z - lax.rem(holder1, nz) + nz, nz)
    mine = pl.ds(pl.multiple_of(x * rows, rows), rows)
    pan[mine, 0:BLK] = zs[back0, 0:rows, 0:BLK]
    pan[mine, BLK : 2 * BLK] = zs[back1, 0:rows, BLK : 2 * BLK]
    fb[core, x] = zs[back1, rows:piece, :]

    sends = []
    for d in range(1, nx):
        copy = pltpu.make_async_remote_copy(
            src_ref=pan.at[mine, :],
            dst_ref=pan.at[mine, :],
            send_sem=psend.at[d],
            recv_sem=precv.at[d],
            device_id={"stn": along_x(d)},
            device_id_type=MESH,
        )
        copy.start()
        sends.append(copy)
    for flip in range(2):
        for d in range(nx):
            if flip or d:
                copy = pltpu.make_async_remote_copy(
                    src_ref=fb.at[core, x],
                    dst_ref=fb.at[core, x],
                    send_sem=fsend.at[flip, d],
                    recv_sem=frecv.at[flip, d],
                    device_id={"stn": along_x(d), "tm": other if flip else tm},
                    device_id_type=MESH,
                )
                copy.start()
                sends.append(copy)

    def drain(step, _):
        for c in range(chunks):
            for way in range(2):
                hop(way, step, c).wait_send()
        return 0

    lax.fori_loop(0, half - 1, drain, 0)
    for way in range(2):
        for c in last(way):
            hop(way, half - 1, c).wait_send()
    for copy in sends:
        copy.wait()
    p_ref[...] = pan[...]
    for side in range(2):
        for q in range(nx):
            lines = fb.shape[2]
            start = side * lines * nx + q * lines
            f_ref[start : start + lines, :] = fb[side, q]


def spread(candidates, panel_block, nx, nz, blocks):
    piece = candidates.shape[1]
    chunks = piece // CHUNK
    frows = BLK // 4 // nx
    half = nz // 2
    vmem = pl.BlockSpec(memory_space=pltpu.VMEM)
    dma = pltpu.SemaphoreType.DMA
    return pl.pallas_call(
        functools.partial(spread_kernel, nx, nz, blocks),
        out_shape=(
            jax.ShapeDtypeStruct((BLK, 2 * BLK), BF16),
            jax.ShapeDtypeStruct((BLK // 2, 2 * BLK), BF16),
        ),
        in_specs=[pl.BlockSpec(memory_space=pltpu.SMEM), vmem],
        out_specs=(vmem, vmem),
        scratch_shapes=[
            pltpu.VMEM((nx, piece, 2 * BLK), BF16),
            pltpu.VMEM((nz, piece, 2 * BLK), BF16),
            pltpu.VMEM((BLK, 2 * BLK), BF16),
            pltpu.VMEM((2, nx, frows, 2 * BLK), BF16),
            dma,
            dma((nx,)),
            dma((nx,)),
            dma((2, half, chunks)),
            dma((2, half, chunks)),
            dma((nx,)),
            dma((nx,)),
            dma((2, nx)),
            dma((2, nx)),
        ],
        compiler_params=pltpu.CompilerParams(collective_id=0, has_side_effects=True),
        name="spread",
    )(panel_block, candidates)


def permutation(transposed):
    rows = lax.broadcasted_iota(jnp.int32, (BLK, BLK), 1 if transposed else 0)
    cols = lax.broadcasted_iota(jnp.int32, (BLK, BLK), 0 if transposed else 1)
    steps = BLK // SEGS
    hit = cols == steps * lax.rem(rows, SEGS) + lax.div(rows, SEGS)
    return jnp.where(hit, 1.0, 0.0).astype(F32)


def halvings(gaps_ref):
    return jnp.where(gaps_ref[...] == 1, 0.5, 1.0).astype(F32)


def own_halvings(halved_ref, perm):
    tm = lax.axis_index("tm")
    row = jnp.concatenate(
        [halved_ref[pl.ds(2 * tm, 1), :], halved_ref[pl.ds(2 * tm + 1, 1), :]], axis=1
    )
    return dot((perm * row).astype(BF16), jnp.ones((BLK, BLK), BF16))


def shifted(a, by):
    return pltpu.roll(a, by, axis=0)


def seg_product(sp_ref):
    total = sp_ref[0:SEGS, :]
    for k in range(1, BLK // SEGS):
        total = total * sp_ref[SEGS * k : SEGS * (k + 1), :]
    return total


def local_kernel(
    pb_ref, panel_ref, f10_ref, diag_ref, r_ref, fc_ref, rate_ref, gaps_ref,
    w_ref, yx_ref, zx_ref, st_ref,
    perm_ref, hl_ref, s_ref, halved_ref, sp_ref, q_ref,
):
    i = pl.program_id(0)

    @pl.when(i == 0)
    def _():
        perm = permutation(False)
        perm_ref[...] = perm.astype(BF16)
        halved_ref[...] = halvings(gaps_ref)
        sp_ref[...] = own_halvings(halved_ref, perm)
        q_ref[...] = seg_product(sp_ref)
        panel = dot(perm_ref[...], panel_ref[...])
        first = panel[:, 0:BLK].astype(BF16)
        second = panel[:, BLK : 2 * BLK]
        solved = sum(dot_t(first, part) for part in reversed(split3(diag_ref[0])))
        s_ref[0] = solved
        parts = split3(solved)
        hl_ref[0:BLK, 0:BLK] = parts[0]
        hl_ref[BLK : 2 * BLK, 0:BLK] = parts[1]
        quarter = BLK // 4
        for n in range(4):
            side, col = n // 2, n % 2
            f10 = f10_ref[
                side * quarter : (side + 1) * quarter, BLK * col : BLK * (col + 1)
            ]
            s_ref[1, :, quarter * n : quarter * (n + 1)] = sum(
                dot_t(part, f10) for part in reversed(parts)
            )
        solved = lax.dot_general(
            second - s_ref[1],
            diag_ref[1],
            (((1,), (1,)), ((), ())),
            precision=lax.Precision.HIGHEST,
            preferred_element_type=F32,
        )
        s_ref[1] = solved
        parts = split3(solved)
        hl_ref[0:BLK, BLK : 2 * BLK] = parts[0]
        hl_ref[BLK : 2 * BLK, BLK : 2 * BLK] = parts[1]

    rel = lax.axis_index("stn") * pl.num_programs(0) + i - pb_ref[0]
    raw = dot(perm_ref[...], r_ref[...])
    both = dot_t(hl_ref[...], fc_ref[...])
    lower = raw - (both[0:BLK] + both[BLK : 2 * BLK])
    w_ref[...] = jnp.where(
        rel >= 2, lower, jnp.where(rel == 1, s_ref[1], jnp.where(rel == 0, s_ref[0], raw))
    )

    rate = rate_ref[...]
    e = jnp.broadcast_to(jnp.exp(-rate), (SEGS, BLK))
    y = jnp.zeros((SEGS, BLK), F32)
    z = jnp.zeros((SEGS, BLK), F32)
    for k in range(BLK // SEGS):
        a = e * sp_ref[SEGS * k : SEGS * (k + 1), :]
        z = a * (z + y)
        y = a * y + w_ref[SEGS * k : SEGS * (k + 1), :]

    seg = lax.broadcasted_iota(jnp.int32, (SEGS, BLK), 0)
    window = q_ref[...]
    by, steps = 1, BLK // SEGS
    while by < SEGS:
        f = jnp.where(seg >= by, window * jnp.exp(-(float(steps) * rate)), 0.0)
        ys, zs = shifted(y, by), shifted(z, by)
        z = z + f * (zs + float(steps) * ys)
        y = y + f * ys
        window = window * shifted(window, by)
        by, steps = by * 2, steps * 2
    st_ref[0:1, :] = y[SEGS - 1 : SEGS, :]
    st_ref[1:2, :] = z[SEGS - 1 : SEGS, :]
    yx_ref[...] = jnp.where(seg >= 1, shifted(y, 1), 0.0)
    zx_ref[...] = jnp.where(seg >= 1, shifted(z, 1), 0.0)


def local(panel, f10, diag, right_sides, factor_cols, rates, gaps, panel_block):
    time_rows, stations = right_sides.shape
    tile = pl.BlockSpec((time_rows, BLK), lambda i: (0, i))
    line = pl.BlockSpec((SEGS, BLK), lambda i: (0, i))

    def whole(shape):
        return pl.BlockSpec(shape, lambda i: (0,) * len(shape))

    return pl.pallas_call(
        local_kernel,
        grid=(stations // BLK,),
        out_shape=(
            jax.ShapeDtypeStruct((time_rows, stations), F32),
            jax.ShapeDtypeStruct((SEGS, stations), F32),
            jax.ShapeDtypeStruct((SEGS, stations), F32),
            jax.ShapeDtypeStruct((2, stations), F32),
        ),
        in_specs=[
            pl.BlockSpec(memory_space=pltpu.SMEM),
            whole(panel.shape),
            whole(f10.shape),
            whole(diag.shape),
            tile,
            pl.BlockSpec((BLK, 2 * BLK), lambda i: (i, 0)),
            pl.BlockSpec((1, BLK), lambda i: (0, i)),
            whole(gaps.shape),
        ],
        out_specs=(tile, line, line, pl.BlockSpec((2, BLK), lambda i: (0, i))),
        scratch_shapes=[
            pltpu.VMEM((BLK, BLK), BF16),
            pltpu.VMEM((2 * BLK, 2 * BLK), BF16),
            pltpu.VMEM((2, BLK, BLK), F32),
            pltpu.VMEM(gaps.shape, F32),
            pltpu.VMEM((BLK, BLK), F32),
            pltpu.VMEM((SEGS, BLK), F32),
        ],
        name="local",
    )(panel_block, panel, f10, diag, right_sides, factor_cols, rates, gaps)


def states_kernel(nt, st_ref, all_ref, buf, own_sem, send, recv):
    tm = lax.axis_index("tm")
    barrier = pltpu.get_barrier_semaphore()
    for d in range(1, nt):
        pl.semaphore_signal(
            barrier, inc=1, device_id={"tm": lax.rem(tm + d, nt)}, device_id_type=MESH
        )
    pl.semaphore_wait(barrier, nt - 1)
    own = pltpu.make_async_copy(st_ref, buf.at[0], own_sem)
    own.start()
    copies = []
    for d in range(1, nt):
        copy = pltpu.make_async_remote_copy(
            src_ref=st_ref,
            dst_ref=buf.at[d],
            send_sem=send.at[d],
            recv_sem=recv.at[d],
            device_id={"tm": lax.rem(tm + d, nt)},
            device_id_type=MESH,
        )
        copy.start()
        copies.append(copy)
    own.wait()
    for copy in copies:
        copy.wait()
    all_ref[...] = buf[...]


def states(st, nt):
    vmem = pl.BlockSpec(memory_space=pltpu.VMEM)
    dma = pltpu.SemaphoreType.DMA
    return pl.pallas_call(
        functools.partial(states_kernel, nt),
        out_shape=jax.ShapeDtypeStruct((nt,) + st.shape, F32),
        in_specs=[vmem],
        out_specs=vmem,
        scratch_shapes=[pltpu.VMEM((nt,) + st.shape, F32), dma, dma((nt,)), dma((nt,))],
        compiler_params=pltpu.CompilerParams(collective_id=1, has_side_effects=True),
        name="states",
    )(st)


def final_kernel(
    nt, w_ref, yx_ref, zx_ref, all_ref, rate_ref, gaps_ref, o_ref,
    back_ref, halved_ref, sp_ref, g_ref, product_ref, level_ref,
):
    tm = lax.axis_index("tm")

    @pl.when(pl.program_id(0) == 0)
    def _():
        back_ref[...] = permutation(True).astype(BF16)
        halved = halvings(gaps_ref)
        halved_ref[...] = halved
        sp_ref[...] = own_halvings(halved_ref, permutation(False))
        by = 1
        while by < 128:
            halved = halved * pltpu.roll(halved, by, axis=1)
            by *= 2
        product_ref[...] = halved
        seg = lax.broadcasted_iota(jnp.int32, (SEGS, BLK), 0)
        g = jnp.where(seg >= 1, shifted(seg_product(sp_ref), 1), 1.0)
        by = 1
        while by < SEGS:
            g = g * jnp.where(seg >= by, shifted(g, by), 1.0)
            by *= 2
        g_ref[...] = g

    rate = rate_ref[...]
    block_decay = jnp.exp(-(float(BLK) * rate))
    y = jnp.zeros((1, BLK), F32)
    z = jnp.zeros((1, BLK), F32)
    for b in range(nt - 1):
        slot = lax.rem(tm - b + nt, nt)
        product = product_ref[2 * b : 2 * b + 1, :] * product_ref[2 * b + 1 : 2 * b + 2, :]
        f = block_decay * jnp.concatenate([product, product], axis=1)
        here = b < tm
        znew = f * (z + float(BLK) * y) + all_ref[slot, 1:2, :]
        ynew = f * y + all_ref[slot, 0:1, :]
        z = jnp.where(here, znew, z)
        y = jnp.where(here, ynew, y)

    seg = lax.broadcasted_iota(jnp.int32, (SEGS, BLK), 0)
    ahead = (seg * (BLK // SEGS)).astype(F32)
    f = g_ref[...] * jnp.exp(-(ahead * rate))
    z = zx_ref[...] + f * (z + ahead * y)
    y = yx_ref[...] + f * y
    e = jnp.broadcast_to(jnp.exp(-rate), (SEGS, BLK))
    gain = jnp.broadcast_to(2.0 * rate * jnp.sqrt(rate), (SEGS, BLK))
    for k in range(BLK // SEGS):
        a = e * sp_ref[SEGS * k : SEGS * (k + 1), :]
        z = a * (z + y)
        y = a * y + w_ref[SEGS * k : SEGS * (k + 1), :]
        level_ref[SEGS * k : SEGS * (k + 1), :] = gain * z
    o_ref[...] = dot(back_ref[...], level_ref[...].astype(BF16)).astype(BF16)


def final(w, yx, zx, everyone, rates, gaps):
    time_rows, stations = w.shape
    nt = everyone.shape[0]
    tile = pl.BlockSpec((time_rows, BLK), lambda i: (0, i))
    line = pl.BlockSpec((SEGS, BLK), lambda i: (0, i))
    return pl.pallas_call(
        functools.partial(final_kernel, nt),
        grid=(stations // BLK,),
        out_shape=jax.ShapeDtypeStruct((time_rows, stations), BF16),
        in_specs=[
            tile,
            line,
            line,
            pl.BlockSpec((nt, 2, BLK), lambda i: (0, 0, i)),
            pl.BlockSpec((1, BLK), lambda i: (0, i)),
            pl.BlockSpec(gaps.shape, lambda i: (0, 0)),
        ],
        out_specs=tile,
        scratch_shapes=[
            pltpu.VMEM((BLK, BLK), BF16),
            pltpu.VMEM(gaps.shape, F32),
            pltpu.VMEM((BLK, BLK), F32),
            pltpu.VMEM((SEGS, BLK), F32),
            pltpu.VMEM(gaps.shape, F32),
            pltpu.VMEM((BLK, BLK), F32),
        ],
        name="final",
    )(w, yx, zx, everyone, rates, gaps)


def on_device(nx, nz, nt, right_sides, factor_cols, diag_inverses, panel_block, decay_rate, gaps):
    stations = right_sides.shape[1]
    rates = decay_rate.reshape(1, stations)
    gaps = gaps.reshape(-1, 128)
    candidates = pick(right_sides, factor_cols, panel_block, nx)
    panel, f10 = spread(candidates, panel_block, nx, nz, stations // BLK)
    w, yx, zx, st = local(
        panel, f10, diag_inverses, right_sides, factor_cols, rates, gaps, panel_block
    )
    return final(w, yx, zx, states(st, nt), rates, gaps)


def solution(mesh):
    nz = RING
    nx = mesh.shape["stn"] // nz
    return jax.shard_map(
        functools.partial(on_device, nx, nz, mesh.shape["tm"]),
        mesh=mesh,
        in_specs=(P("tm", "stn"), P("stn", None), P(), P(), P("stn"), P()),
        out_specs=P("tm", "stn"),
        check_vma=False,
    )
```

```python
import functools

import jax
import jax.numpy as jnp
from jax import lax
from jax.experimental import pallas as pl
from jax.experimental.pallas import tpu as pltpu
from jax.sharding import PartitionSpec as P

MESH = pl.DeviceIdType.MESH
BLK = 256
TILE = 1024
SEGS = 8
RING = 16
PIECES = 5
FROM_ROOT = (6, -6, 3, -3, 1, -1)
REACH = (1, -1, 2, -2, 3, -3, 6, -6)
X_ORDER = {2: (1,), 4: (2, 1, 3)}
F32 = jnp.float32
BF16 = jnp.bfloat16


def dot(a, b):
    return lax.dot_general(a, b, (((1,), (0,)), ((), ())), preferred_element_type=F32)


def dot_t(a, b):
    return lax.dot_general(a, b, (((1,), (1,)), ((), ())), preferred_element_type=F32)


def split3(a):
    high = a.astype(BF16)
    rest = a - high.astype(F32)
    mid = rest.astype(BF16)
    return high, mid, (rest - mid.astype(F32)).astype(BF16)


def pick_kernel(nx, pb_ref, r0_ref, r1_ref, f_ref, c_ref):
    core = lax.rem(lax.axis_index("tm"), 2)
    lines = BLK // 2 // nx
    for q in range(nx):
        for n in range(2):
            rows = slice(lines * (2 * q + n), lines * (2 * q + n + 1))
            c_ref[q, n] = r0_ref[rows, :]
            c_ref[q, 2 + n] = r1_ref[rows, :]
        start = pl.multiple_of(core * (BLK // 2) + lines * q, lines)
        c_ref[q, 4] = f_ref[pl.ds(start, lines), :]


def pick(right_sides, factor_cols, panel_block, nx):
    blocks = right_sides.shape[1] // BLK
    shape = (nx, PIECES, BLK // 2 // nx, BLK)
    return pl.pallas_call(
        functools.partial(pick_kernel, nx),
        out_shape=jax.ShapeDtypeStruct(shape, BF16),
        grid_spec=pltpu.PrefetchScalarGridSpec(
            num_scalar_prefetch=1,
            grid=(1,),
            in_specs=[
                pl.BlockSpec((BLK, BLK), lambda i, pb: (0, lax.rem(pb[0], blocks))),
                pl.BlockSpec((BLK, BLK), lambda i, pb: (0, lax.rem(pb[0] + 1, blocks))),
                pl.BlockSpec((BLK, BLK), lambda i, pb: (lax.rem(pb[0] + 1, blocks), 0)),
            ],
            out_specs=pl.BlockSpec(shape, lambda i, pb: (0, 0, 0, 0)),
        ),
        name="pick",
    )(panel_block, right_sides, right_sides, factor_cols)


def spread_kernel(
    nx, nz, blocks, roots, pb_ref, c_ref, p_ref, f_ref,
    xs, pan, xsend, xrecv, zsend, zrecv, psend, precv, fsend, frecv,
):
    me, tm = lax.axis_index("stn"), lax.axis_index("tm")
    x, z = me // nz, lax.rem(me, nz)
    core = lax.rem(tm, 2)
    other = tm + 1 - 2 * core

    def along_x(d):
        return {"stn": lax.rem(x + d, nx) * nz + z}

    def along_z(d):
        return {"stn": x * nz + lax.rem(z + d + nz, nz)}

    def across(d):
        return dict(along_x(d), tm=other)

    greeted = [along_z(d) for d in REACH] + [across(d) for d in range(nx)]
    greeted += [along_x(d) for d in range(1, nx)]
    barrier = pltpu.get_barrier_semaphore()
    for where in greeted:
        pl.semaphore_signal(barrier, inc=1, device_id=where, device_id_type=MESH)
    pl.semaphore_wait(barrier, len(greeted))

    def remote(src, dst, send, recv, where):
        return pltpu.make_async_remote_copy(
            src_ref=src, dst_ref=dst, send_sem=send, recv_sem=recv,
            device_id=where, device_id_type=MESH,
        )

    def held(c):
        return pan.at[c + (c // 4) * core, x]

    def x_hop(d, c):
        src = c_ref.at[lax.rem(x + d, nx), c]
        return remote(src, xs.at[d, c], xsend.at[d, c], xrecv.at[d, c], along_x(d))

    def z_hop(n, d, c):
        return remote(held(c), held(c), zsend.at[n, c], zrecv.at[c], along_z(d))

    def p_hop(d, c):
        return remote(held(c), held(c), psend.at[d, c], precv.at[d, c], along_x(d))

    def f_hop(d):
        return remote(held(4), held(4), fsend.at[d], frecv.at[d], across(d))

    def share(c, do):
        for d in X_ORDER[nx]:
            do(p_hop(d, c))
        if c == 4:
            for d in range(nx):
                do(f_hop(d))

    def forward(rel, c, place, count, do):
        @pl.when((rel == 3) | (rel == 6) | (rel == nz - 3) | (rel == nz - 6))
        def _():
            do(z_hop(0, 1, c))
            do(z_hop(1, -1, c))

        early = 2 * place < count

        @pl.when((rel == 6) & early)
        def _():
            do(z_hop(2, 2, c))

        @pl.when((rel == nz - 6) & jnp.logical_not(early))
        def _():
            do(z_hop(2, -2, c))

    def each(pieces, do):
        def step(c, _):
            do(c)
            return 0

        lax.fori_loop(pieces[0], pieces[-1] + 1, step, 0)

    def start(copy):
        copy.start()

    def sent(copy):
        copy.wait_send()

    block = pb_ref[0]
    groups = [(roots[0], (0, 1)), (roots[1], (2, 3, 4))]
    if roots[0] == roots[1]:
        groups = [(roots[0], (0, 1, 2, 3, 4))]
    for root, pieces in groups:
        rel = lax.rem(z - root + nz, nz)

        @pl.when(rel == 0)
        def _():
            def offer(c):
                for d in X_ORDER[nx]:
                    x_hop(d, c).start()
                xs[0, c] = c_ref[x, c]

            each(pieces, offer)
            for c in pieces:
                holder = (block if c < 2 else block + 1) // blocks
                slot = lax.rem(x - holder // nz + nx, nx)
                for d in X_ORDER[nx]:
                    x_hop(d, c).wait_recv()
                chosen = xs[0, c]
                for d in range(1, nx):
                    chosen = jnp.where(slot == d, xs[d, c], chosen)
                pan[c if c < 4 else 4 + core, x] = chosen
                for n in range(2):
                    z_hop(n, FROM_ROOT[n], c).start()
            for n in range(2, len(FROM_ROOT)):
                for c in pieces:
                    z_hop(n, FROM_ROOT[n], c).start()
            for c in pieces:
                share(c, start)

        @pl.when(rel != 0)
        def _():
            for place, c in enumerate(pieces):
                z_hop(0, 1, c).wait_recv()
                forward(rel, c, place, len(pieces), start)
                share(c, start)

    for root, pieces in groups:
        rel = lax.rem(z - root + nz, nz)

        @pl.when(rel == 0)
        def _():
            def root_sent(c):
                for d in X_ORDER[nx]:
                    x_hop(d, c).wait_send()
                for n in range(len(FROM_ROOT)):
                    z_hop(n, FROM_ROOT[n], c).wait_send()

            each(pieces, root_sent)

        @pl.when(rel != 0)
        def _():
            each(pieces, lambda c: forward(rel, c, c - pieces[0], len(pieces), sent))

    def shared(c):
        for d in X_ORDER[nx]:
            p_hop(d, c).wait()

    each(range(PIECES), shared)
    for d in range(nx):
        f_hop(d).wait()

    lines = pan.shape[2]
    for q in range(nx):
        for n in range(2):
            rows = slice(lines * (2 * q + n), lines * (2 * q + n + 1))
            p_ref[0, rows, :] = pan[n, q]
            p_ref[1, rows, :] = pan[2 + n, q]
            rows = slice(lines * (nx * n + q), lines * (nx * n + q + 1))
            f_ref[rows, :] = pan[4 + n, q]


def spread(nx, nz, blocks, roots, cid, candidates, panel_block):
    vmem = pl.BlockSpec(memory_space=pltpu.VMEM)
    dma = pltpu.SemaphoreType.DMA
    lines = candidates.shape[2]
    return pl.pallas_call(
        functools.partial(spread_kernel, nx, nz, blocks, roots),
        out_shape=(
            jax.ShapeDtypeStruct((2, BLK, BLK), BF16),
            jax.ShapeDtypeStruct((BLK, BLK), BF16),
        ),
        in_specs=[pl.BlockSpec(memory_space=pltpu.SMEM), vmem],
        out_specs=(vmem, vmem),
        scratch_shapes=[
            pltpu.VMEM(candidates.shape, BF16),
            pltpu.VMEM((PIECES + 1, nx, lines, BLK), BF16),
            dma((nx, PIECES)),
            dma((nx, PIECES)),
            dma((len(FROM_ROOT), PIECES)),
            dma((PIECES,)),
            dma((nx, PIECES)),
            dma((nx, PIECES)),
            dma((nx,)),
            dma((nx,)),
        ],
        compiler_params=pltpu.CompilerParams(collective_id=cid, has_side_effects=True),
        name=f"spread_{roots[0]}_{roots[1]}",
    )(panel_block, candidates)


def spread_from(nx, nz, blocks, candidates, panel_block):
    branches = []
    for apart in range(2):
        for root in range(nz):
            roots = (root, (root + apart) % nz)
            branches.append(
                functools.partial(spread, nx, nz, blocks, roots, 1 + len(branches))
            )
    holder = panel_block[0] // blocks
    apart = (panel_block[0] + 1) // blocks - holder
    return lax.switch(apart * nz + lax.rem(holder, nz), branches, candidates, panel_block)


def permutation(transposed):
    rows = lax.broadcasted_iota(jnp.int32, (BLK, BLK), 1 if transposed else 0)
    cols = lax.broadcasted_iota(jnp.int32, (BLK, BLK), 0 if transposed else 1)
    steps = BLK // SEGS
    hit = cols == steps * lax.rem(rows, SEGS) + lax.div(rows, SEGS)
    return jnp.where(hit, 1.0, 0.0).astype(F32)


def halvings(gaps_ref):
    return jnp.where(gaps_ref[...] == 1, 0.5, 1.0).astype(F32)


def own_halvings(halved_ref, perm):
    tm = lax.axis_index("tm")
    row = jnp.concatenate(
        [halved_ref[pl.ds(2 * tm, 1), :], halved_ref[pl.ds(2 * tm + 1, 1), :]], axis=1
    )
    return dot((perm * row).astype(BF16), jnp.ones((BLK, 128), BF16))


def shifted(a, by):
    return pltpu.roll(a, by, axis=0)


def widened(a):
    return jnp.concatenate([a] * (TILE // 128), axis=1)


def seg_product(sp_ref):
    total = sp_ref[0:SEGS, :]
    for k in range(1, BLK // SEGS):
        total = total * sp_ref[SEGS * k : SEGS * (k + 1), :]
    return total


def local_kernel(
    pb_ref, panel_ref, f10_ref, diag_ref, r_ref, fc_ref, rate_ref, gaps_ref,
    w_ref, yx_ref, zx_ref, st_ref,
    perm_ref, hl_ref, s_ref, halved_ref, sp_ref, q_ref,
):
    i = pl.program_id(0)

    @pl.when(i == 0)
    def _():
        perm = permutation(False)
        perm_ref[...] = perm.astype(BF16)
        halved_ref[...] = halvings(gaps_ref)
        sp_ref[...] = own_halvings(halved_ref, perm)
        q_ref[...] = seg_product(sp_ref)
        first = dot(perm_ref[...], panel_ref[0]).astype(BF16)
        second = dot(perm_ref[...], panel_ref[1])
        solved = sum(dot_t(first, part) for part in reversed(split3(diag_ref[0])))
        s_ref[0] = solved
        parts = split3(solved)
        hl_ref[0:BLK, 0:BLK] = parts[0]
        hl_ref[BLK : 2 * BLK, 0:BLK] = parts[1]
        coupled = sum(dot_t(part, f10_ref[...]) for part in reversed(parts))
        solved = lax.dot_general(
            second - coupled,
            diag_ref[1],
            (((1,), (1,)), ((), ())),
            precision=lax.Precision.HIGHEST,
            preferred_element_type=F32,
        )
        s_ref[1] = solved
        parts = split3(solved)
        hl_ref[0:BLK, BLK : 2 * BLK] = parts[0]
        hl_ref[BLK : 2 * BLK, BLK : 2 * BLK] = parts[1]

    for n in range(TILE // BLK):
        cols = slice(BLK * n, BLK * (n + 1))
        rel = (lax.axis_index("stn") * pl.num_programs(0) + i) * (TILE // BLK) + n - pb_ref[0]
        raw = dot(perm_ref[...], r_ref[:, cols])
        both = dot_t(hl_ref[...], fc_ref[cols, :])
        lower = raw - (both[0:BLK] + both[BLK : 2 * BLK])
        w_ref[:, cols] = jnp.where(
            rel >= 2, lower, jnp.where(rel == 1, s_ref[1], jnp.where(rel == 0, s_ref[0], raw))
        )

    rate = rate_ref[...]
    e = jnp.broadcast_to(jnp.exp(-rate), (SEGS, TILE))
    y = jnp.zeros((SEGS, TILE), F32)
    z = jnp.zeros((SEGS, TILE), F32)
    for k in range(BLK // SEGS):
        a = e * widened(sp_ref[SEGS * k : SEGS * (k + 1), :])
        z = a * (z + y)
        y = a * y + w_ref[SEGS * k : SEGS * (k + 1), :]

    seg = lax.broadcasted_iota(jnp.int32, (SEGS, TILE), 0)
    window = widened(q_ref[...])
    by, steps = 1, BLK // SEGS
    while by < SEGS:
        f = jnp.where(seg >= by, window * jnp.exp(-(float(steps) * rate)), 0.0)
        ys, zs = shifted(y, by), shifted(z, by)
        z = z + f * (zs + float(steps) * ys)
        y = y + f * ys
        window = window * shifted(window, by)
        by, steps = by * 2, steps * 2
    st_ref[0:1, :] = y[SEGS - 1 : SEGS, :]
    st_ref[1:2, :] = z[SEGS - 1 : SEGS, :]
    yx_ref[...] = jnp.where(seg >= 1, shifted(y, 1), 0.0)
    zx_ref[...] = jnp.where(seg >= 1, shifted(z, 1), 0.0)


def local(panel, f10, diag, right_sides, factor_cols, rates, gaps, panel_block):
    time_rows, stations = right_sides.shape
    tile = pl.BlockSpec((time_rows, TILE), lambda i: (0, i))
    line = pl.BlockSpec((SEGS, TILE), lambda i: (0, i))

    def whole(shape):
        return pl.BlockSpec(shape, lambda i: (0,) * len(shape))

    return pl.pallas_call(
        local_kernel,
        grid=(stations // TILE,),
        out_shape=(
            jax.ShapeDtypeStruct((time_rows, stations), F32),
            jax.ShapeDtypeStruct((SEGS, stations), F32),
            jax.ShapeDtypeStruct((SEGS, stations), F32),
            jax.ShapeDtypeStruct((2, stations), F32),
        ),
        in_specs=[
            pl.BlockSpec(memory_space=pltpu.SMEM),
            whole(panel.shape),
            whole(f10.shape),
            whole(diag.shape),
            tile,
            pl.BlockSpec((TILE, 2 * BLK), lambda i: (i, 0)),
            pl.BlockSpec((1, TILE), lambda i: (0, i)),
            whole(gaps.shape),
        ],
        out_specs=(tile, line, line, pl.BlockSpec((2, TILE), lambda i: (0, i))),
        scratch_shapes=[
            pltpu.VMEM((BLK, BLK), BF16),
            pltpu.VMEM((2 * BLK, 2 * BLK), BF16),
            pltpu.VMEM((2, BLK, BLK), F32),
            pltpu.VMEM(gaps.shape, F32),
            pltpu.VMEM((BLK, 128), F32),
            pltpu.VMEM((SEGS, 128), F32),
        ],
        name="local",
    )(panel_block, panel, f10, diag, right_sides, factor_cols, rates, gaps)


def states_kernel(nt, st_ref, all_ref, buf, own_sem, send, recv):
    tm = lax.axis_index("tm")
    barrier = pltpu.get_barrier_semaphore()
    for d in range(1, nt):
        pl.semaphore_signal(
            barrier, inc=1, device_id={"tm": lax.rem(tm + d, nt)}, device_id_type=MESH
        )
    pl.semaphore_wait(barrier, nt - 1)
    own = pltpu.make_async_copy(st_ref, buf.at[0], own_sem)
    own.start()
    copies = []
    for d in range(1, nt):
        copy = pltpu.make_async_remote_copy(
            src_ref=st_ref,
            dst_ref=buf.at[d],
            send_sem=send.at[d],
            recv_sem=recv.at[d],
            device_id={"tm": lax.rem(tm + d, nt)},
            device_id_type=MESH,
        )
        copy.start()
        copies.append(copy)
    own.wait()
    for copy in copies:
        copy.wait()
    all_ref[...] = buf[...]


def states(st, nt):
    vmem = pl.BlockSpec(memory_space=pltpu.VMEM)
    dma = pltpu.SemaphoreType.DMA
    return pl.pallas_call(
        functools.partial(states_kernel, nt),
        out_shape=jax.ShapeDtypeStruct((nt,) + st.shape, F32),
        in_specs=[vmem],
        out_specs=vmem,
        scratch_shapes=[pltpu.VMEM((nt,) + st.shape, F32), dma, dma((nt,)), dma((nt,))],
        compiler_params=pltpu.CompilerParams(collective_id=0, has_side_effects=True),
        name="states",
    )(st)


def final_kernel(
    nt, w_ref, yx_ref, zx_ref, all_ref, rate_ref, gaps_ref, o_ref,
    back_ref, halved_ref, sp_ref, g_ref, product_ref, level_ref,
):
    tm = lax.axis_index("tm")

    @pl.when(pl.program_id(0) == 0)
    def _():
        back_ref[...] = permutation(True).astype(BF16)
        halved = halvings(gaps_ref)
        halved_ref[...] = halved
        sp_ref[...] = own_halvings(halved_ref, permutation(False))
        by = 1
        while by < 128:
            halved = halved * pltpu.roll(halved, by, axis=1)
            by *= 2
        product_ref[...] = halved
        seg = lax.broadcasted_iota(jnp.int32, (SEGS, 128), 0)
        g = jnp.where(seg >= 1, shifted(seg_product(sp_ref), 1), 1.0)
        by = 1
        while by < SEGS:
            g = g * jnp.where(seg >= by, shifted(g, by), 1.0)
            by *= 2
        g_ref[...] = g

    rate = rate_ref[...]
    block_decay = jnp.exp(-(float(BLK) * rate))
    y = jnp.zeros((1, TILE), F32)
    z = jnp.zeros((1, TILE), F32)
    for b in range(nt - 1):
        slot = lax.rem(tm - b + nt, nt)
        product = product_ref[2 * b : 2 * b + 1, :] * product_ref[2 * b + 1 : 2 * b + 2, :]
        f = block_decay * widened(product)
        here = b < tm
        znew = f * (z + float(BLK) * y) + all_ref[slot, 1:2, :]
        ynew = f * y + all_ref[slot, 0:1, :]
        z = jnp.where(here, znew, z)
        y = jnp.where(here, ynew, y)

    seg = lax.broadcasted_iota(jnp.int32, (SEGS, TILE), 0)
    ahead = (seg * (BLK // SEGS)).astype(F32)
    f = widened(g_ref[...]) * jnp.exp(-(ahead * rate))
    z = zx_ref[...] + f * (z + ahead * y)
    y = yx_ref[...] + f * y
    e = jnp.broadcast_to(jnp.exp(-rate), (SEGS, TILE))
    gain = jnp.broadcast_to(2.0 * rate * jnp.sqrt(rate), (SEGS, TILE))
    for k in range(BLK // SEGS):
        a = e * widened(sp_ref[SEGS * k : SEGS * (k + 1), :])
        z = a * (z + y)
        y = a * y + w_ref[SEGS * k : SEGS * (k + 1), :]
        level_ref[SEGS * k : SEGS * (k + 1), :] = gain * z
    for n in range(TILE // BLK):
        cols = slice(BLK * n, BLK * (n + 1))
        o_ref[:, cols] = dot(back_ref[...], level_ref[:, cols].astype(BF16)).astype(BF16)


def final(w, yx, zx, everyone, rates, gaps):
    time_rows, stations = w.shape
    nt = everyone.shape[0]
    tile = pl.BlockSpec((time_rows, TILE), lambda i: (0, i))
    line = pl.BlockSpec((SEGS, TILE), lambda i: (0, i))
    return pl.pallas_call(
        functools.partial(final_kernel, nt),
        grid=(stations // TILE,),
        out_shape=jax.ShapeDtypeStruct((time_rows, stations), BF16),
        in_specs=[
            tile,
            line,
            line,
            pl.BlockSpec((nt, 2, TILE), lambda i: (0, 0, i)),
            pl.BlockSpec((1, TILE), lambda i: (0, i)),
            pl.BlockSpec(gaps.shape, lambda i: (0, 0)),
        ],
        out_specs=tile,
        scratch_shapes=[
            pltpu.VMEM((BLK, BLK), BF16),
            pltpu.VMEM(gaps.shape, F32),
            pltpu.VMEM((BLK, 128), F32),
            pltpu.VMEM((SEGS, 128), F32),
            pltpu.VMEM(gaps.shape, F32),
            pltpu.VMEM((BLK, TILE), F32),
        ],
        name="final",
    )(w, yx, zx, everyone, rates, gaps)


def on_device(nx, nz, nt, right_sides, factor_cols, diag_inverses, panel_block, decay_rate, gaps):
    stations = right_sides.shape[1]
    rates = decay_rate.reshape(1, stations)
    gaps = gaps.reshape(-1, 128)
    candidates = pick(right_sides, factor_cols, panel_block, nx)
    panel, f10 = spread_from(nx, nz, stations // BLK, candidates, panel_block)
    w, yx, zx, st = local(
        panel, f10, diag_inverses, right_sides, factor_cols, rates, gaps, panel_block
    )
    return final(w, yx, zx, states(st, nt), rates, gaps)


def solution(mesh):
    nz = RING
    nx = mesh.shape["stn"] // nz
    return jax.shard_map(
        functools.partial(on_device, nx, nz, mesh.shape["tm"]),
        mesh=mesh,
        in_specs=(P("tm", "stn"), P("stn", None), P(), P(), P("stn"), P()),
        out_specs=P("tm", "stn"),
        check_vma=False,
    )
```

```python
import functools

import jax
import jax.numpy as jnp
from jax import lax
from jax.experimental import pallas as pl
from jax.experimental.pallas import tpu as pltpu
from jax.sharding import PartitionSpec as P

MESH = pl.DeviceIdType.MESH
BLK = 256
TILE = 1024
SEGS = 8
RING = 16
PIECES = 5
PICK_VMEM = 66_400_000
FROM_ROOT = (6, -6, 3, -3, 1, -1)
REACH = (1, -1, 2, -2, 3, -3, 6, -6)
X_ORDER = {2: (1,), 4: (2, 1, 3)}
F32 = jnp.float32
BF16 = jnp.bfloat16


def dot(a, b):
    return lax.dot_general(a, b, (((1,), (0,)), ((), ())), preferred_element_type=F32)


def dot_t(a, b):
    return lax.dot_general(a, b, (((1,), (1,)), ((), ())), preferred_element_type=F32)


def split3(a):
    high = a.astype(BF16)
    rest = a - high.astype(F32)
    mid = rest.astype(BF16)
    return high, mid, (rest - mid.astype(F32)).astype(BF16)


def pick_kernel(nx, pb_ref, r0_ref, r1_ref, f_ref, c_ref):
    core = lax.rem(lax.axis_index("tm"), 2)
    lines = BLK // 2 // nx
    for q in range(nx):
        for n in range(2):
            rows = slice(lines * (2 * q + n), lines * (2 * q + n + 1))
            c_ref[q, n] = r0_ref[rows, :]
            c_ref[q, 2 + n] = r1_ref[rows, :]
        start = pl.multiple_of(core * (BLK // 2) + lines * q, lines)
        c_ref[q, 4] = f_ref[pl.ds(start, lines), :]


def pick(right_sides, factor_cols, panel_block, nx):
    blocks = right_sides.shape[1] // BLK
    shape = (nx, PIECES, BLK // 2 // nx, BLK)
    return pl.pallas_call(
        functools.partial(pick_kernel, nx),
        out_shape=jax.ShapeDtypeStruct(shape, BF16),
        grid_spec=pltpu.PrefetchScalarGridSpec(
            num_scalar_prefetch=1,
            grid=(1,),
            in_specs=[
                pl.BlockSpec((BLK, BLK), lambda i, pb: (0, lax.rem(pb[0], blocks))),
                pl.BlockSpec((BLK, BLK), lambda i, pb: (0, lax.rem(pb[0] + 1, blocks))),
                pl.BlockSpec((BLK, BLK), lambda i, pb: (lax.rem(pb[0] + 1, blocks), 0)),
            ],
            out_specs=pl.BlockSpec(shape, lambda i, pb: (0, 0, 0, 0)),
        ),
        compiler_params=pltpu.CompilerParams(vmem_limit_bytes=PICK_VMEM),
        name="pick",
    )(panel_block, right_sides, right_sides, factor_cols)


def spread_kernel(
    nx, nz, blocks, roots, pb_ref, c_ref, p_ref, f_ref,
    xs, pan, xsend, xrecv, zsend, zrecv, psend, precv, fsend, frecv,
):
    me, tm = lax.axis_index("stn"), lax.axis_index("tm")
    x, z = me // nz, lax.rem(me, nz)
    core = lax.rem(tm, 2)
    other = tm + 1 - 2 * core

    def along_x(d):
        return {"stn": lax.rem(x + d, nx) * nz + z}

    def along_z(d):
        return {"stn": x * nz + lax.rem(z + d + nz, nz)}

    def across(d):
        return dict(along_x(d), tm=other)

    greeted = [along_z(d) for d in REACH] + [across(d) for d in range(nx)]
    greeted += [along_x(d) for d in range(1, nx)]
    barrier = pltpu.get_barrier_semaphore()
    for where in greeted:
        pl.semaphore_signal(barrier, inc=1, device_id=where, device_id_type=MESH)
    pl.semaphore_wait(barrier, len(greeted))

    def remote(src, dst, send, recv, where):
        return pltpu.make_async_remote_copy(
            src_ref=src, dst_ref=dst, send_sem=send, recv_sem=recv,
            device_id=where, device_id_type=MESH,
        )

    def held(c):
        return pan.at[c + (c // 4) * core, x]

    def x_hop(d, c):
        src = c_ref.at[lax.rem(x + d, nx), c]
        return remote(src, xs.at[d, c], xsend.at[d, c], xrecv.at[d, c], along_x(d))

    def z_hop(n, d, c):
        return remote(held(c), held(c), zsend.at[n, c], zrecv.at[c], along_z(d))

    def p_hop(d, c):
        return remote(held(c), held(c), psend.at[d, c], precv.at[d, c], along_x(d))

    def f_hop(d):
        return remote(held(4), held(4), fsend.at[d], frecv.at[d], across(d))

    def share(c, do):
        for d in X_ORDER[nx]:
            do(p_hop(d, c))

    def share_factor(do):
        for d in range(nx):
            do(f_hop(d))

    def forward(rel, c, place, count, do):
        @pl.when((rel == 3) | (rel == 6) | (rel == nz - 3) | (rel == nz - 6))
        def _():
            do(z_hop(0, 1, c))
            do(z_hop(1, -1, c))

        early = 2 * place < count

        @pl.when((rel == 6) & early)
        def _():
            do(z_hop(2, 2, c))

        @pl.when((rel == nz - 6) & jnp.logical_not(early))
        def _():
            do(z_hop(2, -2, c))

    def each(pieces, do):
        def step(c, _):
            do(c)
            return 0

        lax.fori_loop(pieces[0], pieces[-1] + 1, step, 0)

    def start(copy):
        copy.start()

    def sent(copy):
        copy.wait_send()

    block = pb_ref[0]
    groups = [(roots[0], (0, 1)), (roots[1], (2, 3, 4))]
    if roots[0] == roots[1]:
        groups = [(roots[0], (0, 1, 2, 3, 4))]
    for root, pieces in groups:
        rel = lax.rem(z - root + nz, nz)

        @pl.when(rel == 0)
        def _():
            def offer(c):
                for d in X_ORDER[nx]:
                    x_hop(d, c).start()
                xs[0, c] = c_ref[x, c]

            each(pieces, offer)

            def gather(c):
                holder = jnp.where(c < 2, block, block + 1) // blocks
                slot = lax.rem(x - holder // nz + nx, nx)
                for d in X_ORDER[nx]:
                    x_hop(d, c).wait_recv()
                chosen = xs[0, c]
                for d in range(1, nx):
                    chosen = jnp.where(slot == d, xs[d, c], chosen)
                pan[c + (c // 4) * core, x] = chosen
                for n in range(2):
                    z_hop(n, FROM_ROOT[n], c).start()

            each(pieces, gather)
            for n in range(2, len(FROM_ROOT)):
                each(pieces, lambda c: z_hop(n, FROM_ROOT[n], c).start())
            each(pieces, lambda c: share(c, start))

        @pl.when(rel != 0)
        def _():
            def relay(c):
                z_hop(0, 1, c).wait_recv()
                forward(rel, c, c - pieces[0], len(pieces), start)
                share(c, start)

            each(pieces, relay)

    share_factor(start)
    for root, pieces in groups:
        rel = lax.rem(z - root + nz, nz)

        @pl.when(rel == 0)
        def _():
            def root_sent(c):
                for d in X_ORDER[nx]:
                    x_hop(d, c).wait_send()
                for n in range(len(FROM_ROOT)):
                    z_hop(n, FROM_ROOT[n], c).wait_send()

            each(pieces, root_sent)

        @pl.when(rel != 0)
        def _():
            each(pieces, lambda c: forward(rel, c, c - pieces[0], len(pieces), sent))

    def shared(c):
        for d in X_ORDER[nx]:
            p_hop(d, c).wait()

    each(range(PIECES), shared)
    for d in range(nx):
        f_hop(d).wait()

    lines = pan.shape[2]
    for q in range(nx):
        for n in range(2):
            rows = slice(lines * (2 * q + n), lines * (2 * q + n + 1))
            p_ref[0, rows, :] = pan[n, q]
            p_ref[1, rows, :] = pan[2 + n, q]
            rows = slice(lines * (nx * n + q), lines * (nx * n + q + 1))
            f_ref[rows, :] = pan[4 + n, q]


def spread(nx, nz, blocks, roots, cid, candidates, panel_block):
    vmem = pl.BlockSpec(memory_space=pltpu.VMEM)
    dma = pltpu.SemaphoreType.DMA
    lines = candidates.shape[2]
    return pl.pallas_call(
        functools.partial(spread_kernel, nx, nz, blocks, roots),
        out_shape=(
            jax.ShapeDtypeStruct((2, BLK, BLK), BF16),
            jax.ShapeDtypeStruct((BLK, BLK), BF16),
        ),
        in_specs=[pl.BlockSpec(memory_space=pltpu.SMEM), vmem],
        out_specs=(vmem, vmem),
        scratch_shapes=[
            pltpu.VMEM(candidates.shape, BF16),
            pltpu.VMEM((PIECES + 1, nx, lines, BLK), BF16),
            dma((nx, PIECES)),
            dma((nx, PIECES)),
            dma((len(FROM_ROOT), PIECES)),
            dma((PIECES,)),
            dma((nx, PIECES)),
            dma((nx, PIECES)),
            dma((nx,)),
            dma((nx,)),
        ],
        compiler_params=pltpu.CompilerParams(
            collective_id=cid, has_side_effects=True, vmem_limit_bytes=4 << 20
        ),
        name=f"spread_{roots[0]}_{roots[1]}",
    )(panel_block, candidates)


def spread_from(nx, nz, blocks, candidates, panel_block):
    branches = []
    for apart in range(2):
        for root in range(nz):
            roots = (root, (root + apart) % nz)
            branches.append(
                functools.partial(spread, nx, nz, blocks, roots, 1 + len(branches))
            )
    holder = panel_block[0] // blocks
    apart = (panel_block[0] + 1) // blocks - holder
    return lax.switch(apart * nz + lax.rem(holder, nz), branches, candidates, panel_block)


def permutation(transposed):
    rows = lax.broadcasted_iota(jnp.int32, (BLK, BLK), 1 if transposed else 0)
    cols = lax.broadcasted_iota(jnp.int32, (BLK, BLK), 0 if transposed else 1)
    steps = BLK // SEGS
    hit = cols == steps * lax.rem(rows, SEGS) + lax.div(rows, SEGS)
    return jnp.where(hit, 1.0, 0.0).astype(F32)


def halvings(gaps_ref):
    return jnp.where(gaps_ref[...] == 1, 0.5, 1.0).astype(F32)


def own_halvings(halved_ref, perm):
    tm = lax.axis_index("tm")
    row = jnp.concatenate(
        [halved_ref[pl.ds(2 * tm, 1), :], halved_ref[pl.ds(2 * tm + 1, 1), :]], axis=1
    )
    return dot((perm * row).astype(BF16), jnp.ones((BLK, 128), BF16))


def shifted(a, by):
    return pltpu.roll(a, by, axis=0)


def widened(a):
    return jnp.concatenate([a] * (TILE // 128), axis=1)


def seg_product(sp_ref):
    total = sp_ref[0:SEGS, :]
    for k in range(1, BLK // SEGS):
        total = total * sp_ref[SEGS * k : SEGS * (k + 1), :]
    return total


def local_kernel(
    pb_ref, panel_ref, f10_ref, diag_ref, r_ref, fc_ref, rate_ref, gaps_ref,
    w_ref, yx_ref, zx_ref, st_ref,
    perm_ref, hl_ref, s_ref, halved_ref, sp_ref, q_ref,
):
    i = pl.program_id(0)

    @pl.when(i == 0)
    def _():
        perm = permutation(False)
        perm_ref[...] = perm.astype(BF16)
        halved_ref[...] = halvings(gaps_ref)
        sp_ref[...] = own_halvings(halved_ref, perm)
        q_ref[...] = seg_product(sp_ref)
        first = dot(perm_ref[...], panel_ref[0]).astype(BF16)
        second = dot(perm_ref[...], panel_ref[1])
        solved = sum(dot_t(first, part) for part in reversed(split3(diag_ref[0])))
        s_ref[0] = solved
        parts = split3(solved)
        hl_ref[0:BLK, 0:BLK] = parts[0]
        hl_ref[BLK : 2 * BLK, 0:BLK] = parts[1]
        coupled = sum(dot_t(part, f10_ref[...]) for part in reversed(parts))
        solved = lax.dot_general(
            second - coupled,
            diag_ref[1],
            (((1,), (1,)), ((), ())),
            precision=lax.Precision.HIGHEST,
            preferred_element_type=F32,
        )
        s_ref[1] = solved
        parts = split3(solved)
        hl_ref[0:BLK, BLK : 2 * BLK] = parts[0]
        hl_ref[BLK : 2 * BLK, BLK : 2 * BLK] = parts[1]

    for n in range(TILE // BLK):
        cols = slice(BLK * n, BLK * (n + 1))
        rel = (lax.axis_index("stn") * pl.num_programs(0) + i) * (TILE // BLK) + n - pb_ref[0]
        raw = dot(perm_ref[...], r_ref[:, cols])
        both = dot_t(hl_ref[...], fc_ref[cols, :])
        lower = raw - (both[0:BLK] + both[BLK : 2 * BLK])
        w_ref[:, cols] = jnp.where(
            rel >= 2, lower, jnp.where(rel == 1, s_ref[1], jnp.where(rel == 0, s_ref[0], raw))
        )

    rate = rate_ref[...]
    e = jnp.broadcast_to(jnp.exp(-rate), (SEGS, TILE))
    y = jnp.zeros((SEGS, TILE), F32)
    z = jnp.zeros((SEGS, TILE), F32)
    for k in range(BLK // SEGS):
        a = e * widened(sp_ref[SEGS * k : SEGS * (k + 1), :])
        z = a * (z + y)
        y = a * y + w_ref[SEGS * k : SEGS * (k + 1), :]

    seg = lax.broadcasted_iota(jnp.int32, (SEGS, TILE), 0)
    window = widened(q_ref[...])
    by, steps = 1, BLK // SEGS
    while by < SEGS:
        f = jnp.where(seg >= by, window * jnp.exp(-(float(steps) * rate)), 0.0)
        ys, zs = shifted(y, by), shifted(z, by)
        z = z + f * (zs + float(steps) * ys)
        y = y + f * ys
        window = window * shifted(window, by)
        by, steps = by * 2, steps * 2
    st_ref[0:1, :] = y[SEGS - 1 : SEGS, :]
    st_ref[1:2, :] = z[SEGS - 1 : SEGS, :]
    yx_ref[...] = jnp.where(seg >= 1, shifted(y, 1), 0.0)
    zx_ref[...] = jnp.where(seg >= 1, shifted(z, 1), 0.0)


def local(panel, f10, diag, right_sides, factor_cols, rates, gaps, panel_block):
    time_rows, stations = right_sides.shape
    tile = pl.BlockSpec((time_rows, TILE), lambda i: (0, i))
    line = pl.BlockSpec((SEGS, TILE), lambda i: (0, i))

    def whole(shape):
        return pl.BlockSpec(shape, lambda i: (0,) * len(shape))

    return pl.pallas_call(
        local_kernel,
        grid=(stations // TILE,),
        out_shape=(
            jax.ShapeDtypeStruct((time_rows, stations), F32),
            jax.ShapeDtypeStruct((SEGS, stations), F32),
            jax.ShapeDtypeStruct((SEGS, stations), F32),
            jax.ShapeDtypeStruct((2, stations), F32),
        ),
        in_specs=[
            pl.BlockSpec(memory_space=pltpu.SMEM),
            whole(panel.shape),
            whole(f10.shape),
            whole(diag.shape),
            tile,
            pl.BlockSpec((TILE, 2 * BLK), lambda i: (i, 0)),
            pl.BlockSpec((1, TILE), lambda i: (0, i)),
            whole(gaps.shape),
        ],
        out_specs=(tile, line, line, pl.BlockSpec((2, TILE), lambda i: (0, i))),
        scratch_shapes=[
            pltpu.VMEM((BLK, BLK), BF16),
            pltpu.VMEM((2 * BLK, 2 * BLK), BF16),
            pltpu.VMEM((2, BLK, BLK), F32),
            pltpu.VMEM(gaps.shape, F32),
            pltpu.VMEM((BLK, 128), F32),
            pltpu.VMEM((SEGS, 128), F32),
        ],
        compiler_params=pltpu.CompilerParams(vmem_limit_bytes=16 << 20),
        name="local",
    )(panel_block, panel, f10, diag, right_sides, factor_cols, rates, gaps)


def states_kernel(nt, st_ref, all_ref, buf, own_sem, send, recv):
    tm = lax.axis_index("tm")
    barrier = pltpu.get_barrier_semaphore()
    for d in range(1, nt):
        pl.semaphore_signal(
            barrier, inc=1, device_id={"tm": lax.rem(tm + d, nt)}, device_id_type=MESH
        )
    pl.semaphore_wait(barrier, nt - 1)
    own = pltpu.make_async_copy(st_ref, buf.at[0], own_sem)
    own.start()
    copies = []
    for d in range(1, nt):
        copy = pltpu.make_async_remote_copy(
            src_ref=st_ref,
            dst_ref=buf.at[d],
            send_sem=send.at[d],
            recv_sem=recv.at[d],
            device_id={"tm": lax.rem(tm + d, nt)},
            device_id_type=MESH,
        )
        copy.start()
        copies.append(copy)
    own.wait()
    for copy in copies:
        copy.wait()
    all_ref[...] = buf[...]


def states(st, nt):
    vmem = pl.BlockSpec(memory_space=pltpu.VMEM)
    dma = pltpu.SemaphoreType.DMA
    return pl.pallas_call(
        functools.partial(states_kernel, nt),
        out_shape=jax.ShapeDtypeStruct((nt,) + st.shape, F32),
        in_specs=[vmem],
        out_specs=vmem,
        scratch_shapes=[pltpu.VMEM((nt,) + st.shape, F32), dma, dma((nt,)), dma((nt,))],
        compiler_params=pltpu.CompilerParams(
            collective_id=0, has_side_effects=True, vmem_limit_bytes=4 << 20
        ),
        name="states",
    )(st)


def final_kernel(
    nt, w_ref, yx_ref, zx_ref, all_ref, rate_ref, gaps_ref, o_ref,
    back_ref, halved_ref, sp_ref, g_ref, product_ref, level_ref,
):
    tm = lax.axis_index("tm")

    @pl.when(pl.program_id(0) == 0)
    def _():
        back_ref[...] = permutation(True).astype(BF16)
        halved = halvings(gaps_ref)
        halved_ref[...] = halved
        sp_ref[...] = own_halvings(halved_ref, permutation(False))
        by = 1
        while by < 128:
            halved = halved * pltpu.roll(halved, by, axis=1)
            by *= 2
        product_ref[...] = halved
        seg = lax.broadcasted_iota(jnp.int32, (SEGS, 128), 0)
        g = jnp.where(seg >= 1, shifted(seg_product(sp_ref), 1), 1.0)
        by = 1
        while by < SEGS:
            g = g * jnp.where(seg >= by, shifted(g, by), 1.0)
            by *= 2
        g_ref[...] = g

    rate = rate_ref[...]
    block_decay = jnp.exp(-(float(BLK) * rate))
    y = jnp.zeros((1, TILE), F32)
    z = jnp.zeros((1, TILE), F32)
    for b in range(nt - 1):
        slot = lax.rem(tm - b + nt, nt)
        product = product_ref[2 * b : 2 * b + 1, :] * product_ref[2 * b + 1 : 2 * b + 2, :]
        f = block_decay * widened(product)
        here = b < tm
        znew = f * (z + float(BLK) * y) + all_ref[slot, 1:2, :]
        ynew = f * y + all_ref[slot, 0:1, :]
        z = jnp.where(here, znew, z)
        y = jnp.where(here, ynew, y)

    seg = lax.broadcasted_iota(jnp.int32, (SEGS, TILE), 0)
    ahead = (seg * (BLK // SEGS)).astype(F32)
    f = widened(g_ref[...]) * jnp.exp(-(ahead * rate))
    z = zx_ref[...] + f * (z + ahead * y)
    y = yx_ref[...] + f * y
    e = jnp.broadcast_to(jnp.exp(-rate), (SEGS, TILE))
    gain = jnp.broadcast_to(2.0 * rate * jnp.sqrt(rate), (SEGS, TILE))
    for k in range(BLK // SEGS):
        a = e * widened(sp_ref[SEGS * k : SEGS * (k + 1), :])
        z = a * (z + y)
        y = a * y + w_ref[SEGS * k : SEGS * (k + 1), :]
        level_ref[SEGS * k : SEGS * (k + 1), :] = gain * z
    for n in range(TILE // BLK):
        cols = slice(BLK * n, BLK * (n + 1))
        o_ref[:, cols] = dot(back_ref[...], level_ref[:, cols].astype(BF16)).astype(BF16)


def final(w, yx, zx, everyone, rates, gaps):
    time_rows, stations = w.shape
    nt = everyone.shape[0]
    tile = pl.BlockSpec((time_rows, TILE), lambda i: (0, i))
    line = pl.BlockSpec((SEGS, TILE), lambda i: (0, i))
    return pl.pallas_call(
        functools.partial(final_kernel, nt),
        grid=(stations // TILE,),
        out_shape=jax.ShapeDtypeStruct((time_rows, stations), BF16),
        in_specs=[
            tile,
            line,
            line,
            pl.BlockSpec((nt, 2, TILE), lambda i: (0, 0, i)),
            pl.BlockSpec((1, TILE), lambda i: (0, i)),
            pl.BlockSpec(gaps.shape, lambda i: (0, 0)),
        ],
        out_specs=tile,
        scratch_shapes=[
            pltpu.VMEM((BLK, BLK), BF16),
            pltpu.VMEM(gaps.shape, F32),
            pltpu.VMEM((BLK, 128), F32),
            pltpu.VMEM((SEGS, 128), F32),
            pltpu.VMEM(gaps.shape, F32),
            pltpu.VMEM((BLK, TILE), F32),
        ],
        compiler_params=pltpu.CompilerParams(vmem_limit_bytes=16 << 20),
        name="final",
    )(w, yx, zx, everyone, rates, gaps)


def on_device(nx, nz, nt, right_sides, factor_cols, diag_inverses, panel_block, decay_rate, gaps):
    stations = right_sides.shape[1]
    rates = decay_rate.reshape(1, stations)
    gaps = gaps.reshape(-1, 128)
    candidates = pick(right_sides, factor_cols, panel_block, nx)
    panel, f10 = spread_from(nx, nz, stations // BLK, candidates, panel_block)
    diag_inverses = pltpu.with_memory_space_constraint(diag_inverses, pltpu.HBM)
    w, yx, zx, st = local(
        panel, f10, diag_inverses, right_sides, factor_cols, rates, gaps, panel_block
    )
    return final(w, yx, zx, states(st, nt), rates, gaps)


def solution(mesh):
    nz = RING
    nx = mesh.shape["stn"] // nz
    return jax.shard_map(
        functools.partial(on_device, nx, nz, mesh.shape["tm"]),
        mesh=mesh,
        in_specs=(P("tm", "stn"), P("stn", None), P(), P(), P("stn"), P()),
        out_specs=P("tm", "stn"),
        check_vma=False,
    )
```

```python
import functools

import jax
import jax.numpy as jnp
from jax import lax
from jax.experimental import pallas as pl
from jax.experimental.pallas import tpu as pltpu
from jax.sharding import PartitionSpec as P

MESH = pl.DeviceIdType.MESH
BLK = 256
TILE = 2048
SEGS = 8
RING = 16
PIECES = 5
PICK_VMEM = 66_400_000
FROM_ROOT = (6, -6, 3, -3, 1, -1)
REACH = (1, -1, 2, -2, 3, -3, 6, -6)
X_ORDER = {2: (1,), 4: (2, 1, 3)}
F32 = jnp.float32
BF16 = jnp.bfloat16


def dot(a, b):
    return lax.dot_general(a, b, (((1,), (0,)), ((), ())), preferred_element_type=F32)


def dot_t(a, b):
    return lax.dot_general(a, b, (((1,), (1,)), ((), ())), preferred_element_type=F32)


def split3(a):
    high = a.astype(BF16)
    rest = a - high.astype(F32)
    mid = rest.astype(BF16)
    return high, mid, (rest - mid.astype(F32)).astype(BF16)


def pick_kernel(nx, pb_ref, r0_ref, r1_ref, f_ref, c_ref):
    core = lax.rem(lax.axis_index("tm"), 2)
    lines = BLK // 2 // nx
    for q in range(nx):
        for n in range(2):
            rows = slice(lines * (2 * q + n), lines * (2 * q + n + 1))
            c_ref[q, n] = r0_ref[rows, :]
            c_ref[q, 2 + n] = r1_ref[rows, :]
        start = pl.multiple_of(core * (BLK // 2) + lines * q, lines)
        c_ref[q, 4] = f_ref[pl.ds(start, lines), :]


def pick(right_sides, factor_cols, panel_block, nx):
    blocks = right_sides.shape[1] // BLK
    shape = (nx, PIECES, BLK // 2 // nx, BLK)
    return pl.pallas_call(
        functools.partial(pick_kernel, nx),
        out_shape=jax.ShapeDtypeStruct(shape, BF16),
        grid_spec=pltpu.PrefetchScalarGridSpec(
            num_scalar_prefetch=1,
            grid=(1,),
            in_specs=[
                pl.BlockSpec((BLK, BLK), lambda i, pb: (0, lax.rem(pb[0], blocks))),
                pl.BlockSpec((BLK, BLK), lambda i, pb: (0, lax.rem(pb[0] + 1, blocks))),
                pl.BlockSpec((BLK, BLK), lambda i, pb: (lax.rem(pb[0] + 1, blocks), 0)),
            ],
            out_specs=pl.BlockSpec(shape, lambda i, pb: (0, 0, 0, 0)),
        ),
        compiler_params=pltpu.CompilerParams(vmem_limit_bytes=PICK_VMEM),
        name="pick",
    )(panel_block, right_sides, right_sides, factor_cols)


def spread_kernel(
    nx, nz, blocks, roots, pb_ref, c_ref, p_ref, f_ref,
    xs, pan, xsend, xrecv, zsend, zrecv, psend, precv, fsend, frecv,
):
    me, tm = lax.axis_index("stn"), lax.axis_index("tm")
    x, z = me // nz, lax.rem(me, nz)
    core = lax.rem(tm, 2)
    other = tm + 1 - 2 * core

    def along_x(d):
        return {"stn": lax.rem(x + d, nx) * nz + z}

    def along_z(d):
        return {"stn": x * nz + lax.rem(z + d + nz, nz)}

    def across(d):
        return dict(along_x(d), tm=other)

    greeted = [along_z(d) for d in REACH] + [across(d) for d in range(nx)]
    greeted += [along_x(d) for d in range(1, nx)]
    barrier = pltpu.get_barrier_semaphore()
    for where in greeted:
        pl.semaphore_signal(barrier, inc=1, device_id=where, device_id_type=MESH)
    pl.semaphore_wait(barrier, len(greeted))

    def remote(src, dst, send, recv, where):
        return pltpu.make_async_remote_copy(
            src_ref=src, dst_ref=dst, send_sem=send, recv_sem=recv,
            device_id=where, device_id_type=MESH,
        )

    def held(c):
        return pan.at[c + (c // 4) * core, x]

    def x_hop(d, c):
        src = c_ref.at[lax.rem(x + d, nx), c]
        return remote(src, xs.at[d, c], xsend.at[d, c], xrecv.at[d, c], along_x(d))

    def z_hop(n, d, c):
        return remote(held(c), held(c), zsend.at[n, c], zrecv.at[c], along_z(d))

    def p_hop(d, c):
        return remote(held(c), held(c), psend.at[d, c], precv.at[d, c], along_x(d))

    def f_hop(d):
        return remote(held(4), held(4), fsend.at[d], frecv.at[d], across(d))

    def share(c, do):
        for d in X_ORDER[nx]:
            do(p_hop(d, c))

    def share_factor(do):
        for d in range(nx):
            do(f_hop(d))

    def forward(rel, c, place, count, do):
        @pl.when((rel == 3) | (rel == 6) | (rel == nz - 3) | (rel == nz - 6))
        def _():
            do(z_hop(0, 1, c))
            do(z_hop(1, -1, c))

        early = 2 * place < count

        @pl.when((rel == 6) & early)
        def _():
            do(z_hop(2, 2, c))

        @pl.when((rel == nz - 6) & jnp.logical_not(early))
        def _():
            do(z_hop(2, -2, c))

    def each(pieces, do):
        def step(c, _):
            do(c)
            return 0

        lax.fori_loop(pieces[0], pieces[-1] + 1, step, 0)

    def start(copy):
        copy.start()

    def sent(copy):
        copy.wait_send()

    block = pb_ref[0]
    groups = [(roots[0], (0, 1)), (roots[1], (2, 3, 4))]
    if roots[0] == roots[1]:
        groups = [(roots[0], (0, 1, 2, 3, 4))]
    for root, pieces in groups:
        rel = lax.rem(z - root + nz, nz)

        @pl.when(rel == 0)
        def _():
            def offer(c):
                for d in X_ORDER[nx]:
                    x_hop(d, c).start()
                xs[0, c] = c_ref[x, c]

            each(pieces, offer)

            def gather(c):
                holder = jnp.where(c < 2, block, block + 1) // blocks
                slot = lax.rem(x - holder // nz + nx, nx)
                for d in X_ORDER[nx]:
                    x_hop(d, c).wait_recv()
                chosen = xs[0, c]
                for d in range(1, nx):
                    chosen = jnp.where(slot == d, xs[d, c], chosen)
                pan[c + (c // 4) * core, x] = chosen
                for n in range(2):
                    z_hop(n, FROM_ROOT[n], c).start()

            each(pieces, gather)
            for n in range(2, len(FROM_ROOT)):
                each(pieces, lambda c: z_hop(n, FROM_ROOT[n], c).start())
            each(pieces, lambda c: share(c, start))

        @pl.when(rel != 0)
        def _():
            def relay(c):
                z_hop(0, 1, c).wait_recv()
                forward(rel, c, c - pieces[0], len(pieces), start)
                share(c, start)

            each(pieces, relay)

    share_factor(start)
    for root, pieces in groups:
        rel = lax.rem(z - root + nz, nz)

        @pl.when(rel == 0)
        def _():
            def root_sent(c):
                for d in X_ORDER[nx]:
                    x_hop(d, c).wait_send()
                for n in range(len(FROM_ROOT)):
                    z_hop(n, FROM_ROOT[n], c).wait_send()

            each(pieces, root_sent)

        @pl.when(rel != 0)
        def _():
            each(pieces, lambda c: forward(rel, c, c - pieces[0], len(pieces), sent))

    def shared(c):
        for d in X_ORDER[nx]:
            p_hop(d, c).wait()

    each(range(PIECES), shared)
    for d in range(nx):
        f_hop(d).wait()

    lines = pan.shape[2]
    for q in range(nx):
        for n in range(2):
            rows = slice(lines * (2 * q + n), lines * (2 * q + n + 1))
            p_ref[0, rows, :] = pan[n, q]
            p_ref[1, rows, :] = pan[2 + n, q]
            rows = slice(lines * (nx * n + q), lines * (nx * n + q + 1))
            f_ref[rows, :] = pan[4 + n, q]


def spread(nx, nz, blocks, roots, cid, candidates, panel_block):
    vmem = pl.BlockSpec(memory_space=pltpu.VMEM)
    dma = pltpu.SemaphoreType.DMA
    lines = candidates.shape[2]
    return pl.pallas_call(
        functools.partial(spread_kernel, nx, nz, blocks, roots),
        out_shape=(
            jax.ShapeDtypeStruct((2, BLK, BLK), BF16),
            jax.ShapeDtypeStruct((BLK, BLK), BF16),
        ),
        in_specs=[pl.BlockSpec(memory_space=pltpu.SMEM), vmem],
        out_specs=(vmem, vmem),
        scratch_shapes=[
            pltpu.VMEM(candidates.shape, BF16),
            pltpu.VMEM((PIECES + 1, nx, lines, BLK), BF16),
            dma((nx, PIECES)),
            dma((nx, PIECES)),
            dma((len(FROM_ROOT), PIECES)),
            dma((PIECES,)),
            dma((nx, PIECES)),
            dma((nx, PIECES)),
            dma((nx,)),
            dma((nx,)),
        ],
        compiler_params=pltpu.CompilerParams(
            collective_id=cid, has_side_effects=True, vmem_limit_bytes=4 << 20
        ),
        name=f"spread_{roots[0]}_{roots[1]}",
    )(panel_block, candidates)


def spread_from(nx, nz, blocks, candidates, panel_block):
    branches = []
    for apart in range(2):
        for root in range(nz):
            roots = (root, (root + apart) % nz)
            branches.append(
                functools.partial(spread, nx, nz, blocks, roots, 1 + len(branches))
            )
    holder = panel_block[0] // blocks
    apart = (panel_block[0] + 1) // blocks - holder
    return lax.switch(apart * nz + lax.rem(holder, nz), branches, candidates, panel_block)


def permutation(transposed):
    rows = lax.broadcasted_iota(jnp.int32, (BLK, BLK), 1 if transposed else 0)
    cols = lax.broadcasted_iota(jnp.int32, (BLK, BLK), 0 if transposed else 1)
    steps = BLK // SEGS
    hit = cols == steps * lax.rem(rows, SEGS) + lax.div(rows, SEGS)
    return jnp.where(hit, 1.0, 0.0).astype(F32)


def halvings(gaps_ref):
    return jnp.where(gaps_ref[...] == 1, 0.5, 1.0).astype(F32)


def own_halvings(halved_ref, perm):
    tm = lax.axis_index("tm")
    row = jnp.concatenate(
        [halved_ref[pl.ds(2 * tm, 1), :], halved_ref[pl.ds(2 * tm + 1, 1), :]], axis=1
    )
    return dot((perm * row).astype(BF16), jnp.ones((BLK, 128), BF16))


def shifted(a, by):
    return pltpu.roll(a, by, axis=0)


def widened(a):
    return jnp.concatenate([a] * (TILE // 128), axis=1)


def seg_product(sp_ref):
    total = sp_ref[0:SEGS, :]
    for k in range(1, BLK // SEGS):
        total = total * sp_ref[SEGS * k : SEGS * (k + 1), :]
    return total


def local_kernel(
    nt, pb_ref, panel_ref, f10_ref, diag_ref, r_ref, fc_ref, rate_ref, gaps_ref,
    w_ref, yx_ref, zx_ref, all_ref,
    perm_ref, hl_ref, s_ref, halved_ref, sp_ref, q_ref, st, buf, send, recv,
):
    i = pl.program_id(0)
    tm = lax.axis_index("tm")
    barrier = pltpu.get_barrier_semaphore()

    @pl.when(i == 0)
    def _():
        for d in range(1, nt):
            pl.semaphore_signal(
                barrier, inc=1, device_id={"tm": lax.rem(tm + d, nt)}, device_id_type=MESH
            )

    @pl.when(i == 0)
    def _():
        perm = permutation(False)
        perm_ref[...] = perm.astype(BF16)
        halved_ref[...] = halvings(gaps_ref)
        sp_ref[...] = own_halvings(halved_ref, perm)
        q_ref[...] = seg_product(sp_ref)
        first = dot(perm_ref[...], panel_ref[0]).astype(BF16)
        second = dot(perm_ref[...], panel_ref[1])
        solved = sum(dot_t(first, part) for part in reversed(split3(diag_ref[0])))
        s_ref[0] = solved
        parts = split3(solved)
        hl_ref[0:BLK, 0:BLK] = parts[0]
        hl_ref[BLK : 2 * BLK, 0:BLK] = parts[1]
        coupled = sum(dot_t(part, f10_ref[...]) for part in reversed(parts))
        solved = lax.dot_general(
            second - coupled,
            diag_ref[1],
            (((1,), (1,)), ((), ())),
            precision=lax.Precision.HIGHEST,
            preferred_element_type=F32,
        )
        s_ref[1] = solved
        parts = split3(solved)
        hl_ref[0:BLK, BLK : 2 * BLK] = parts[0]
        hl_ref[BLK : 2 * BLK, BLK : 2 * BLK] = parts[1]

    for n in range(TILE // BLK):
        cols = slice(BLK * n, BLK * (n + 1))
        rel = (lax.axis_index("stn") * pl.num_programs(0) + i) * (TILE // BLK) + n - pb_ref[0]
        raw = dot(perm_ref[...], r_ref[:, cols])
        both = dot_t(hl_ref[...], fc_ref[cols, :])
        lower = raw - (both[0:BLK] + both[BLK : 2 * BLK])
        w_ref[:, cols] = jnp.where(
            rel >= 2, lower, jnp.where(rel == 1, s_ref[1], jnp.where(rel == 0, s_ref[0], raw))
        )

    rate = rate_ref[...]
    e = jnp.broadcast_to(jnp.exp(-rate), (SEGS, TILE))
    y = jnp.zeros((SEGS, TILE), F32)
    z = jnp.zeros((SEGS, TILE), F32)
    for k in range(BLK // SEGS):
        a = e * widened(sp_ref[SEGS * k : SEGS * (k + 1), :])
        z = a * (z + y)
        y = a * y + w_ref[SEGS * k : SEGS * (k + 1), :]

    seg = lax.broadcasted_iota(jnp.int32, (SEGS, TILE), 0)
    window = widened(q_ref[...])
    by, steps = 1, BLK // SEGS
    while by < SEGS:
        f = jnp.where(seg >= by, window * jnp.exp(-(float(steps) * rate)), 0.0)
        ys, zs = shifted(y, by), shifted(z, by)
        z = z + f * (zs + float(steps) * ys)
        y = y + f * ys
        window = window * shifted(window, by)
        by, steps = by * 2, steps * 2
    cols = pl.ds(pl.multiple_of(i * TILE, TILE), TILE)
    st[0:1, cols] = y[SEGS - 1 : SEGS, :]
    st[1:2, cols] = z[SEGS - 1 : SEGS, :]
    yx_ref[...] = jnp.where(seg >= 1, shifted(y, 1), 0.0)
    zx_ref[...] = jnp.where(seg >= 1, shifted(z, 1), 0.0)

    @pl.when(i == pl.num_programs(0) - 1)
    def _():
        pl.semaphore_wait(barrier, nt - 1)
        copies = []
        for d in range(1, nt):
            copy = pltpu.make_async_remote_copy(
                src_ref=st,
                dst_ref=buf.at[d],
                send_sem=send.at[d],
                recv_sem=recv.at[d],
                device_id={"tm": lax.rem(tm + d, nt)},
                device_id_type=MESH,
            )
            copy.start()
            copies.append(copy)
        all_ref[0] = st[...]
        for d, copy in enumerate(copies):
            copy.wait()
            all_ref[d + 1] = buf[d + 1]


def local(nt, panel, f10, diag, right_sides, factor_cols, rates, gaps, panel_block):
    time_rows, stations = right_sides.shape
    tile = pl.BlockSpec((time_rows, TILE), lambda i: (0, i))
    line = pl.BlockSpec((SEGS, TILE), lambda i: (0, i))

    def whole(shape):
        return pl.BlockSpec(shape, lambda i: (0,) * len(shape))

    return pl.pallas_call(
        functools.partial(local_kernel, nt),
        grid=(stations // TILE,),
        out_shape=(
            jax.ShapeDtypeStruct((time_rows, stations), F32),
            jax.ShapeDtypeStruct((SEGS, stations), F32),
            jax.ShapeDtypeStruct((SEGS, stations), F32),
            jax.ShapeDtypeStruct((nt, 2, stations), F32),
        ),
        in_specs=[
            pl.BlockSpec(memory_space=pltpu.SMEM),
            whole(panel.shape),
            whole(f10.shape),
            whole(diag.shape),
            tile,
            pl.BlockSpec((TILE, 2 * BLK), lambda i: (i, 0)),
            pl.BlockSpec((1, TILE), lambda i: (0, i)),
            whole(gaps.shape),
        ],
        out_specs=(tile, line, line, whole((nt, 2, stations))),
        scratch_shapes=[
            pltpu.VMEM((BLK, BLK), BF16),
            pltpu.VMEM((2 * BLK, 2 * BLK), BF16),
            pltpu.VMEM((2, BLK, BLK), F32),
            pltpu.VMEM(gaps.shape, F32),
            pltpu.VMEM((BLK, 128), F32),
            pltpu.VMEM((SEGS, 128), F32),
            pltpu.VMEM((2, stations), F32),
            pltpu.VMEM((nt, 2, stations), F32),
            pltpu.SemaphoreType.DMA((nt,)),
            pltpu.SemaphoreType.DMA((nt,)),
        ],
        compiler_params=pltpu.CompilerParams(
            collective_id=0, has_side_effects=True, vmem_limit_bytes=16 << 20
        ),
        name="local",
    )(panel_block, panel, f10, diag, right_sides, factor_cols, rates, gaps)


def final_kernel(
    nt, w_ref, yx_ref, zx_ref, all_ref, rate_ref, gaps_ref, o_ref,
    back_ref, halved_ref, sp_ref, g_ref, product_ref, level_ref,
):
    tm = lax.axis_index("tm")

    @pl.when(pl.program_id(0) == 0)
    def _():
        back_ref[...] = permutation(True).astype(BF16)
        halved = halvings(gaps_ref)
        halved_ref[...] = halved
        sp_ref[...] = own_halvings(halved_ref, permutation(False))
        by = 1
        while by < 128:
            halved = halved * pltpu.roll(halved, by, axis=1)
            by *= 2
        product_ref[...] = halved
        seg = lax.broadcasted_iota(jnp.int32, (SEGS, 128), 0)
        g = jnp.where(seg >= 1, shifted(seg_product(sp_ref), 1), 1.0)
        by = 1
        while by < SEGS:
            g = g * jnp.where(seg >= by, shifted(g, by), 1.0)
            by *= 2
        g_ref[...] = g

    rate = rate_ref[...]
    block_decay = jnp.exp(-(float(BLK) * rate))
    y = jnp.zeros((1, TILE), F32)
    z = jnp.zeros((1, TILE), F32)
    for b in range(nt - 1):
        slot = lax.rem(tm - b + nt, nt)
        product = product_ref[2 * b : 2 * b + 1, :] * product_ref[2 * b + 1 : 2 * b + 2, :]
        f = block_decay * widened(product)
        here = b < tm
        znew = f * (z + float(BLK) * y) + all_ref[slot, 1:2, :]
        ynew = f * y + all_ref[slot, 0:1, :]
        z = jnp.where(here, znew, z)
        y = jnp.where(here, ynew, y)

    seg = lax.broadcasted_iota(jnp.int32, (SEGS, TILE), 0)
    ahead = (seg * (BLK // SEGS)).astype(F32)
    f = widened(g_ref[...]) * jnp.exp(-(ahead * rate))
    z = zx_ref[...] + f * (z + ahead * y)
    y = yx_ref[...] + f * y
    e = jnp.broadcast_to(jnp.exp(-rate), (SEGS, TILE))
    gain = jnp.broadcast_to(2.0 * rate * jnp.sqrt(rate), (SEGS, TILE))
    for k in range(BLK // SEGS):
        a = e * widened(sp_ref[SEGS * k : SEGS * (k + 1), :])
        z = a * (z + y)
        y = a * y + w_ref[SEGS * k : SEGS * (k + 1), :]
        level_ref[SEGS * k : SEGS * (k + 1), :] = gain * z
    for n in range(TILE // BLK):
        cols = slice(BLK * n, BLK * (n + 1))
        o_ref[:, cols] = dot(back_ref[...], level_ref[:, cols].astype(BF16)).astype(BF16)


def final(w, yx, zx, everyone, rates, gaps):
    time_rows, stations = w.shape
    nt = everyone.shape[0]
    tile = pl.BlockSpec((time_rows, TILE), lambda i: (0, i))
    line = pl.BlockSpec((SEGS, TILE), lambda i: (0, i))
    return pl.pallas_call(
        functools.partial(final_kernel, nt),
        grid=(stations // TILE,),
        out_shape=jax.ShapeDtypeStruct((time_rows, stations), BF16),
        in_specs=[
            tile,
            line,
            line,
            pl.BlockSpec((nt, 2, TILE), lambda i: (0, 0, i)),
            pl.BlockSpec((1, TILE), lambda i: (0, i)),
            pl.BlockSpec(gaps.shape, lambda i: (0, 0)),
        ],
        out_specs=tile,
        scratch_shapes=[
            pltpu.VMEM((BLK, BLK), BF16),
            pltpu.VMEM(gaps.shape, F32),
            pltpu.VMEM((BLK, 128), F32),
            pltpu.VMEM((SEGS, 128), F32),
            pltpu.VMEM(gaps.shape, F32),
            pltpu.VMEM((BLK, TILE), F32),
        ],
        compiler_params=pltpu.CompilerParams(vmem_limit_bytes=16 << 20),
        name="final",
    )(w, yx, zx, everyone, rates, gaps)


def on_device(nx, nz, nt, right_sides, factor_cols, diag_inverses, panel_block, decay_rate, gaps):
    stations = right_sides.shape[1]
    rates = decay_rate.reshape(1, stations)
    gaps = gaps.reshape(-1, 128)
    candidates = pick(right_sides, factor_cols, panel_block, nx)
    panel, f10 = spread_from(nx, nz, stations // BLK, candidates, panel_block)
    diag_inverses = pltpu.with_memory_space_constraint(diag_inverses, pltpu.HBM)
    w, yx, zx, everyone = local(
        nt, panel, f10, diag_inverses, right_sides, factor_cols, rates, gaps, panel_block
    )
    return final(w, yx, zx, everyone, rates, gaps)


def solution(mesh):
    nz = RING
    nx = mesh.shape["stn"] // nz
    return jax.shard_map(
        functools.partial(on_device, nx, nz, mesh.shape["tm"]),
        mesh=mesh,
        in_specs=(P("tm", "stn"), P("stn", None), P(), P(), P("stn"), P()),
        out_specs=P("tm", "stn"),
        check_vma=False,
    )
```
